32 devices in a mesh: swath: 2 (over x), band: 16 (over z, y, core).
Axes of the slice: x: 2, y: 2, z: 4, core: 2. Of those that a mesh axis runs over, the one named last changes fastest.
Arguments:
- design: bfloat16 [512, 16384], P(('swath', 'band')), parts along dimension 0, may hold values from 0 to 1
- row_taps: bfloat16 [8, 33], replicated, may hold values from -1 to 1
- column_taps: bfloat16 [8, 33], replicated, may hold values from -1 to 1
- kernel_weight: float32 [8], replicated, may hold values from 0.5 to 2
- interp: bfloat16 [32, 8], replicated, may hold values from 0 to 0.29882812
- block_shift: int32 [2, 4, 16], P(None, 'swath', 'band'), parts along dimension 1, may hold values from -24 to 24
- block_phase: int32 [2, 4, 16], P(None, 'swath', 'band'), parts along dimension 1, may hold values from 0 to 31
- care: int32 [4, 16], P('swath', 'band'), parts along dimension 0, may hold values 0 or 1
- image: bfloat16 [512, 16384], P('swath', 'band'), parts along dimension 0, may hold values from 0 to 20, as said below
Outputs:
- diff_map: bfloat16 [512, 16384], P('swath', 'band'), parts along dimension 0
The draws below stay inside these ranges and needn't reach their ends.
There are 2 independent parts, one for each index of `swath`. The reference program is written for one: setup_inputs(seed, part) draws one part's arguments, and reference() takes and returns one part's arrays. A program takes and returns all parts, laid end to end along the dimension named above; an argument that names none is the same for every part. Nothing has to cross between parts.
Inputs may be any that keep to these rules, and one draw needn't show every extreme that they name: `image`: nonnegative intensities.
All inputs are finite; a program needn't handle non-finite values. No bound on the sum of `care` on one device may be relied on, other than what follows from the above.
Results may differ from the reference program's by a relative error of at most 0.0045.
Values may be sent and summed in bfloat16 or wider, within the bound.
No kernel may reach another device: no remote copies, remote signals or barrier semaphores. Data moves between devices by JAX's collectives and lax.ppermute only.
A program may use at most 64 MiB of HBM per device.

```python
import math
import jax
import jax.numpy as jnp
from jax import lax

W = 16384
NK = 8
KH = 16
SHIFT = 24
IH = 4
NF = 32
BLK = 128
P_SIZE = 28
H = 256
CW = 1024
BROWS = 2
N_BAND = 16


def draw_image(key, part):
    first = jax.random.fold_in(jax.random.fold_in(key, 7), 0)
    columns = jnp.arange(W, dtype=jnp.float32)
    ramp = 1.0 + 2.0 * columns / (W - 1)
    base = jax.random.uniform(first, (H, W), jnp.float32, 0.5, 1.5)
    return (base * ramp[None, :]).astype(jnp.bfloat16)


def with_ends(values, own_key, smallest, high):
    longest = values.shape.index(max(values.shape))
    spots = []
    for shift in (0, 1):
        where = [jax.random.randint(jax.random.fold_in(own_key, axis), (), 0, length) for axis, length in enumerate(values.shape)]
        where[longest] = (where[longest] + shift) % values.shape[longest]
        spots.append(tuple(where))
    return values.at[spots[0]].set(smallest).at[spots[1]].set(high)


def block_scale(rng, dims, shards, low, top_value):
    def one(dim, blocks):
        heights = jax.random.uniform(jax.random.fold_in(jax.random.fold_in(rng, 6), dim), (blocks,), jnp.float32, low / len(shards), top_value / len(shards))
        return jnp.repeat(jnp.exp(heights), dims[dim] // blocks).reshape((-1,) + (1,) * (len(dims) - dim - 1))

    level = one(*shards[0])
    for cut in shards[1:]:
        level = level * one(*cut)
    return level


def normal_values(rng, extent, width, bound, held_as=jnp.bfloat16):
    values = jax.random.normal(rng, extent, jnp.float32) * width
    return jnp.minimum(jnp.maximum(values, -bound), bound).astype(held_as)


def setup_inputs(seed: int = 0, part: int = 0) -> dict:
    arg_keys = jax.random.split(jax.random.key(seed), 10)
    part_splits = jax.random.split(jax.random.fold_in(arg_keys[9], part), 10)
    design = jnp.clip(1.0 * jax.random.uniform(part_splits[0], (H, W), jnp.float32) ** block_scale(part_splits[0], (H, W), ((0, 16),), -0.2, 0.2), 0.0, 1.0).astype(jnp.bfloat16)
    row_taps = normal_values(arg_keys[1], (NK, 2 * KH + 1), (2 * KH + 1) ** -0.5, 1.0)
    column_taps = normal_values(arg_keys[2], (NK, 2 * KH + 1), (2 * KH + 1) ** -0.5, 1.0)
    kernel_weight = jnp.clip(jnp.exp(jax.random.uniform(arg_keys[3], (NK,), jnp.float32, math.log(0.5), math.log(2.0))), 0.5, 2.0)
    interp = jnp.clip(jax.random.uniform(arg_keys[4], (NF, 2 * IH), jnp.float32, 0.0, 0.29882812), 0.0, 0.29882812).astype(jnp.bfloat16)
    block_shift = with_ends(jax.random.randint(part_splits[5], (2, BROWS, N_BAND), -SHIFT, SHIFT + 1), jax.random.fold_in(part_splits[5], 1), -SHIFT, SHIFT).astype(jnp.int32)
    block_phase = with_ends(jax.random.randint(part_splits[6], (2, BROWS, N_BAND), 0, NF), jax.random.fold_in(part_splits[6], 1), 0, NF - 1).astype(jnp.int32)
    care = with_ends((jax.random.randint(part_splits[7], (BROWS, N_BAND), 0, 3) < 2).astype(jnp.int32), jax.random.fold_in(part_splits[7], 1), 0, 1)
    image = draw_image(jax.random.fold_in(jax.random.fold_in(arg_keys[9], part), 71), part)
    return {"design": design, "row_taps": row_taps, "column_taps": column_taps, "kernel_weight": kernel_weight, "interp": interp, "block_shift": block_shift, "block_phase": block_phase, "care": care, "image": image}


epsilon = 1e-05

def band_matrix(offsets, phases, interp, size_out, size_in):
    table = jax.nn.one_hot(phases, NF, dtype=jnp.float32)
    weights = jnp.dot(table, interp.astype(jnp.float32), precision=lax.Precision.HIGHEST)
    outer = jnp.arange(size_out, dtype=jnp.int32)
    inner = jnp.arange(size_in, dtype=jnp.int32)
    position = inner[None, None, :] - outer[None, :, None] - offsets[:, None, None] + (IH - 1 - P_SIZE)
    matrix = jnp.zeros(position.shape, jnp.float32)
    for tap in range(2 * IH):
        matrix = matrix + jnp.where(position == tap, weights[:, tap][:, None, None], 0.0)
    return matrix.astype(jnp.bfloat16)

def warp_strip(framed, shifts, phases, interp):
    height = framed.shape[0] - BLK - 2 * P_SIZE
    across = framed.shape[1]
    strip_cols = across - 2 * P_SIZE
    count = height // BLK
    upper = framed[:height].reshape(count, BLK, across)[:, :P_SIZE]
    middle = framed[P_SIZE:P_SIZE + height].reshape(count, BLK, across)
    lower = framed[BLK + P_SIZE:BLK + P_SIZE + height].reshape(count, BLK, across)[:, :P_SIZE]
    blocks = jnp.concatenate([upper, middle, lower], axis=1)
    row_matrix = band_matrix(shifts[0], phases[0], interp, BLK, BLK + 2 * P_SIZE)
    column_matrix = band_matrix(shifts[1], phases[1], interp, strip_cols, across)
    partial_value = jnp.einsum('brs,bsc->brc', row_matrix.astype(jnp.float32), blocks.astype(jnp.float32), precision=lax.Precision.HIGHEST).astype(jnp.bfloat16)
    return jnp.einsum('brs,bcs->brc', partial_value.astype(jnp.float32), column_matrix.astype(jnp.float32), precision=lax.Precision.HIGHEST)

def finish(warped, strip, cares):
    count, rows, cols = warped.shape
    measured = strip.reshape(count, rows, cols).astype(jnp.float32)
    difference = (cares.astype(jnp.float32)[:, None, None] * (measured - warped)).reshape(count * rows, cols)
    padded = jnp.pad(difference, ((1, 1), (0, 0)))
    return difference + 0.5 * (padded[:-2] + padded[2:])

def reference(design, row_taps, column_taps, kernel_weight, interp, block_shift, block_phase, care, image):
    plane = design.astype(jnp.float32)[None, None]

    def add_kernel(kernel, total):
        row_filter = row_taps[kernel].astype(jnp.float32).reshape(1, 1, 2 * KH + 1, 1)
        smoothed = lax.conv_general_dilated(plane, row_filter, (1, 1), ((KH, KH), (0, 0)), precision=lax.Precision.HIGHEST).astype(jnp.bfloat16)
        column_filter = column_taps[kernel].astype(jnp.float32).reshape(1, 1, 1, 2 * KH + 1)
        field = lax.conv_general_dilated(smoothed.astype(jnp.float32), column_filter, (1, 1), ((0, 0), (KH, KH)), precision=lax.Precision.HIGHEST)[0, 0]
        return total + kernel_weight[kernel] * field * field
    total = lax.fori_loop(0, NK, add_kernel, jnp.zeros((H, W), jnp.float32))
    intensity = total.astype(jnp.bfloat16)
    padded = jnp.pad(intensity, ((P_SIZE, BLK + P_SIZE), (P_SIZE, P_SIZE)))
    strips = image.reshape(H, N_BAND, CW).transpose(1, 0, 2)
    starts = (jnp.arange(N_BAND, dtype=jnp.int32) * CW).astype(jnp.int32)

    def one_strip(items):
        start, shifts, phases, cares, strip = items
        framed = lax.dynamic_slice_in_dim(padded, start, CW + 2 * P_SIZE, axis=1)
        warped = warp_strip(framed, shifts, phases, interp)
        return finish(warped, strip, cares)
    filtered = lax.map(one_strip, (starts, jnp.moveaxis(block_shift, 2, 0), jnp.moveaxis(block_phase, 2, 0), care.T, strips))
    cells = H * W
    mean = jnp.sum(filtered) / cells
    variance = jnp.sum((filtered - mean) * (filtered - mean)) / cells
    care_rows = jnp.repeat(care.T.astype(jnp.float32), BLK, axis=1)
    result = care_rows[:, :, None] * (filtered - mean) * lax.rsqrt(variance + epsilon)
    return result.transpose(1, 0, 2).reshape(H, W).astype(jnp.bfloat16)
```

```python
import functools

import jax
import jax.numpy as jnp
from jax import lax
from jax.experimental import pallas as pl
from jax.experimental.pallas import tpu as pltpu
from jax.sharding import PartitionSpec as P

BLK = 128
P_SIZE = 28
LANES = 128
WIN = 256
ZERO = 160

epsilon = 1e-05


class Plan:
    def __init__(self, devices, rows_dev, width, kernels, reach, taps):
        self.devices, self.rows_dev, self.width = devices, rows_dev, width
        self.kernels, self.reach, self.taps = kernels, reach, taps
        self.half = reach // 2
        self.height = rows_dev * devices
        self.strip = width // devices
        self.piece = self.strip + LANES
        self.blocks = self.height // BLK
        self.tile_rows = min(self.height, 256)
        self.row_tiles = self.height // self.tile_rows
        self.pad = 0 if self.row_tiles == 1 else LANES
        self.window = self.tile_rows + 2 * self.pad
        self.step = WIN - 2 * self.half
        self.tile_cols = min(self.strip, 256)
        self.col_tiles = self.strip // self.tile_cols
        self.chunks = pl.cdiv(self.strip + 2 * P_SIZE, self.step)
        self.lead = P_SIZE + self.half
        self.pairs = []
        for q in range(self.col_tiles):
            first = (self.tile_cols * q + 1) // self.step
            last = min((self.tile_cols * (q + 1) - 1 + 2 * P_SIZE) // self.step, self.chunks - 1)
            self.pairs += [(q, c) for c in range(first, last + 1)]
        self.ext = pl.cdiv(LANES + self.step * self.chunks + WIN, LANES) * LANES


def send_kernel(plan, design, out):
    lane = lax.broadcasted_iota(jnp.int32, (plan.rows_dev, LANES), 1)
    zero = jnp.zeros((plan.rows_dev, LANES), design.dtype)
    strip = plan.strip
    for s in range(plan.devices):
        at = s * strip
        out[s, :, :strip] = design[:, at : at + strip]
        before = design[:, at - LANES : at] if s else zero
        after = design[:, at + strip : at + strip + LANES] if s < plan.devices - 1 else zero
        out[s, :, strip:] = jnp.where(lane < LANES // 2, after, before)


def matrix_kernel(
    plan, row_taps, column_taps, interp, shift, phase, rows, columns, up, across, tap_rows, tap_cols, fine, fine_back
):
    wide = 3 * LANES
    for held in (tap_rows, tap_cols, fine, fine_back):
        held[...] = jnp.zeros_like(held)
    tap_rows[:, : plan.reach] = row_taps[...].astype(jnp.float32)
    fine[:, : plan.taps] = interp[...].astype(jnp.float32)
    a = lax.broadcasted_iota(jnp.int32, (LANES, LANES), 0)
    b = lax.broadcasted_iota(jnp.int32, (LANES, LANES), 1)

    def flipped(held, count):
        swap = jnp.where(a + b == count - 1, 1.0, 0.0).astype(jnp.bfloat16)
        return jnp.dot(held[:, :LANES].astype(jnp.bfloat16), swap, preferred_element_type=jnp.float32)

    tap_cols[:, : plan.reach] = column_taps[...].astype(jnp.float32)
    tap_cols[:, :LANES] = flipped(tap_cols, plan.reach)
    fine_back[:, :LANES] = flipped(fine, plan.taps)
    zero = jnp.zeros((16, LANES), jnp.bfloat16)
    row = lax.broadcasted_iota(jnp.int32, (16, wide), 0)

    def tiles(taps, moved):
        base = pltpu.roll(jnp.broadcast_to(taps, (16, wide)), ZERO + moved, 1)
        for bit in (1, 2, 4, 8):
            base = jnp.where((row & bit) != 0, pltpu.roll(base, bit, 1), base)
        return {m - ZERO: base[:, m : m + LANES].astype(jnp.bfloat16) for m in range(16, 208, 16)}

    def toeplitz(out, at, bank, offset, count, cols, used=None):
        for g in range(count // 16):
            for j in range(cols // LANES):
                start = LANES * j - 16 * g - offset
                tile = bank.get(start, zero) if used is None or 16 * g < used else zero
                out[pl.ds(pl.multiple_of(at + 16 * g, 16), 16), LANES * j : LANES * (j + 1)] = tile

    def per_kernel(k, carry):
        bank = tiles(tap_rows[pl.ds(k, 1), :], 0)
        toeplitz(rows, k * plan.tile_rows, bank, plan.pad - plan.half, plan.tile_rows, plan.window)
        bank = tiles(tap_cols[pl.ds(k, 1), :], 0)
        toeplitz(columns, k * WIN, bank, 1 - plan.reach, WIN, WIN)
        return carry

    lax.fori_loop(0, plan.kernels, per_kernel, 0)
    middle = plan.taps // 2 - 1
    for b in range(plan.blocks):
        inside = (b * BLK) % plan.tile_rows
        bank = tiles(fine[pl.ds(phase[0, b, 0], 1), :], shift[0, b, 0] - middle)
        toeplitz(up, b * BLK, bank, plan.pad + inside, BLK, plan.window)
        bank = tiles(fine_back[pl.ds(phase[1, b, 0], 1), :], -shift[1, b, 0])
        for at, (q, c) in enumerate(plan.pairs):
            offset = plan.step * c - plan.tile_cols * q - P_SIZE + middle - (plan.taps - 1)
            toeplitz(across, (b * len(plan.pairs) + at) * WIN, bank, offset, WIN, plan.tile_cols, plan.step)


def main_kernel(
    plan, design, rows, columns, up, across, weight, care, image, filtered, sums, ext, chunk, smooth, intensity, partial, diff
):
    high, pad, tile = plan.height, plan.pad, plan.tile_rows
    strip = plan.strip
    place = lax.axis_index("band")
    if pad:
        ext[...] = jnp.zeros_like(ext)
        intensity[...] = jnp.zeros_like(intensity)
    elif plan.ext > strip + 2 * LANES:
        ext[:, strip + 2 * LANES :] = jnp.zeros((high, plan.ext - strip - 2 * LANES), ext.dtype)
    ext[pad : pad + high, :LANES] = design[:, strip:]
    ext[pad : pad + high, LANES : LANES + strip] = design[:, :strip]
    ext[pad : pad + high, LANES + strip : 2 * LANES + strip] = design[:, strip:]
    for c in range(plan.chunks):
        at = LANES - plan.lead + plan.step * c
        chunk[c] = ext[:, at : at + WIN]

    def render(c, carry):
        column = lax.broadcasted_iota(jnp.int32, (tile, WIN), 1) + (plan.step * c - P_SIZE + place * strip)
        inside = (column >= 0) & (column < plan.width)
        for r in range(plan.row_tiles):
            smooth[...] = jnp.dot(
                rows[...], chunk[c, tile * r : tile * r + plan.window, :], preferred_element_type=jnp.float32
            ).astype(jnp.bfloat16)
            total = jnp.zeros((tile, WIN), jnp.float32)
            for k in range(plan.kernels):
                field = jnp.dot(
                    smooth[tile * k : tile * (k + 1), :],
                    columns[WIN * k : WIN * (k + 1), :],
                    preferred_element_type=jnp.float32,
                )
                total = total + weight[k] * field * field
            intensity[c, pad + tile * r : pad + tile * (r + 1), :] = jnp.where(inside, total, 0.0).astype(jnp.bfloat16)
        for r in range(plan.row_tiles):
            partial[c, tile * r : tile * (r + 1), :] = jnp.dot(
                up[tile * r : tile * (r + 1), :],
                intensity[c, tile * r : tile * r + plan.window, :],
                preferred_element_type=jnp.float32,
            ).astype(jnp.bfloat16)
        return carry

    lax.fori_loop(0, plan.chunks, render, 0)

    diff[:8, :] = jnp.zeros((8, strip), jnp.float32)
    diff[8 + high :, :] = jnp.zeros((8, strip), jnp.float32)
    for b in range(plan.blocks):
        cared = care[b, 0].astype(jnp.float32)
        for q in range(plan.col_tiles):
            warped = jnp.zeros((BLK, plan.tile_cols), jnp.float32)
            for at, (tile_at, c) in enumerate(plan.pairs):
                if tile_at == q:
                    start = (b * len(plan.pairs) + at) * WIN
                    warped = warped + jnp.dot(
                        partial[c, BLK * b : BLK * (b + 1), :],
                        across[start : start + WIN, :],
                        preferred_element_type=jnp.float32,
                    )
            cols = slice(plan.tile_cols * q, plan.tile_cols * (q + 1))
            measured = image[BLK * b : BLK * (b + 1), cols].astype(jnp.float32)
            diff[8 + BLK * b : 8 + BLK * (b + 1), cols] = cared * (measured - warped)
    first = jnp.zeros((8, LANES), jnp.float32)
    second = jnp.zeros((8, LANES), jnp.float32)
    for at in range(0, strip, LANES):
        cols = slice(at, at + LANES)
        value = diff[8 : 8 + high, cols] + 0.5 * (diff[7 : 7 + high, cols] + diff[9 : 9 + high, cols])
        filtered[:, cols] = value
        split = value.reshape(high // 8, 8, LANES)
        first = first + jnp.sum(split, axis=0)
        second = second + jnp.sum(split * split, axis=0)
    sums[0] = first
    sums[1] = second


def last_kernel(plan, filtered, sums, care, out):
    cells = plan.height * plan.width
    mean = jnp.sum(sums[0]) / cells
    variance = jnp.sum(sums[1]) / cells - mean * mean
    scale = lax.rsqrt(jnp.full((1, LANES), variance + epsilon, jnp.float32))
    for b in range(plan.blocks):
        cared = care[b, 0].astype(jnp.float32)
        for at in range(0, plan.strip, LANES):
            value = filtered[BLK * b : BLK * (b + 1), at : at + LANES]
            out[BLK * b : BLK * (b + 1), at : at + LANES] = (cared * ((value - mean) * scale)).astype(out.dtype)


VMEM = pl.BlockSpec(memory_space=pltpu.VMEM)
SMEM = pl.BlockSpec(memory_space=pltpu.SMEM)


def total_over(values, axis):
    count = lax.axis_size(axis)
    if count & (count - 1):
        return lax.psum(values, axis)
    bit = 1
    while bit < count:
        values = values + lax.ppermute(values, axis, [(i, i ^ bit) for i in range(count)])
        bit *= 2
    return values


def on_device(
    design, row_taps, column_taps, kernel_weight, interp, block_shift, block_phase, care, image
):
    plan = Plan(
        lax.axis_size("band"), design.shape[0], design.shape[1], row_taps.shape[0], row_taps.shape[1], interp.shape[1]
    )
    bf16, f32 = jnp.bfloat16, jnp.float32
    high, strip, kernels = plan.height, plan.strip, plan.kernels
    send = pl.pallas_call(
        functools.partial(send_kernel, plan),
        out_shape=jax.ShapeDtypeStruct((plan.devices, plan.rows_dev, plan.piece), bf16),
        in_specs=[VMEM],
        out_specs=VMEM,
    )(design)
    got = lax.all_to_all(send, "band", 0, 0, tiled=True).reshape(high, plan.piece)
    rows, columns, up, across = pl.pallas_call(
        functools.partial(matrix_kernel, plan),
        out_shape=[
            jax.ShapeDtypeStruct((kernels * plan.tile_rows, plan.window), bf16),
            jax.ShapeDtypeStruct((kernels * WIN, WIN), bf16),
            jax.ShapeDtypeStruct((high, plan.window), bf16),
            jax.ShapeDtypeStruct((plan.blocks * len(plan.pairs) * WIN, plan.tile_cols), bf16),
        ],
        in_specs=[VMEM, VMEM, VMEM, SMEM, SMEM],
        out_specs=[VMEM] * 4,
        scratch_shapes=[
            pltpu.VMEM((kernels, 3 * LANES), f32),
            pltpu.VMEM((kernels, 3 * LANES), f32),
            pltpu.VMEM((interp.shape[0], 3 * LANES), f32),
            pltpu.VMEM((interp.shape[0], 3 * LANES), f32),
        ],
        cost_estimate=pl.CostEstimate(flops=10**9, bytes_accessed=8 * 10**6, transcendentals=0),
    )(row_taps, column_taps, interp, block_shift, block_phase)
    filtered, sums = pl.pallas_call(
        functools.partial(main_kernel, plan),
        out_shape=[
            jax.ShapeDtypeStruct((high, strip), f32),
            jax.ShapeDtypeStruct((2, 8, LANES), f32),
        ],
        in_specs=[VMEM] * 5 + [SMEM, SMEM, VMEM],
        out_specs=[VMEM] * 2,
        scratch_shapes=[
            pltpu.VMEM((high + 2 * plan.pad, plan.ext), bf16),
            pltpu.VMEM((plan.chunks, high + 2 * plan.pad, WIN), bf16),
            pltpu.VMEM((kernels * plan.tile_rows, WIN), bf16),
            pltpu.VMEM((plan.chunks, high + 2 * plan.pad, WIN), bf16),
            pltpu.VMEM((plan.chunks, high, WIN), bf16),
            pltpu.VMEM((high + 16, strip), f32),
        ],
        cost_estimate=pl.CostEstimate(flops=4 * 10**9, bytes_accessed=8 * 10**6, transcendentals=0),
    )(got, rows, columns, up, across, kernel_weight, care, image)
    sums = total_over(sums, "band")
    return pl.pallas_call(
        functools.partial(last_kernel, plan),
        out_shape=jax.ShapeDtypeStruct((high, strip), bf16),
        in_specs=[VMEM, VMEM, SMEM],
        out_specs=VMEM,
    )(filtered, sums, care)


def solution(mesh):
    placed = (
        P(("swath", "band"), None),
        P(),
        P(),
        P(),
        P(),
        P(None, "swath", "band"),
        P(None, "swath", "band"),
        P("swath", "band"),
        P("swath", "band"),
    )
    return jax.shard_map(
        on_device, mesh=mesh, in_specs=placed, out_specs=P("swath", "band"), check_vma=False
    )
```

```python
import functools

import jax
import jax.numpy as jnp
from jax import lax
from jax.experimental import pallas as pl
from jax.experimental.pallas import tpu as pltpu
from jax.sharding import PartitionSpec as P

BLK = 128
P_SIZE = 28
LANES = 128
WIN = 256
ZERO = 160
TILES = 12

epsilon = 1e-05


class Plan:
    def __init__(self, devices, rows_dev, width, kernels, reach, taps):
        self.devices, self.rows_dev, self.width = devices, rows_dev, width
        self.kernels, self.reach, self.taps = kernels, reach, taps
        self.half = reach // 2
        self.height = rows_dev * devices
        self.strip = width // devices
        self.piece = self.strip + LANES
        self.blocks = self.height // BLK
        self.tile_rows = min(self.height, 256)
        self.row_tiles = self.height // self.tile_rows
        self.pad = 0 if self.row_tiles == 1 else LANES
        self.window = self.tile_rows + 2 * self.pad
        self.step = WIN - 2 * self.half
        self.tile_cols = min(self.strip, 256)
        self.col_tiles = self.strip // self.tile_cols
        self.chunks = pl.cdiv(self.strip + 2 * P_SIZE, self.step)
        self.lead = P_SIZE + self.half
        self.pairs = []
        for q in range(self.col_tiles):
            first = (self.tile_cols * q + 1) // self.step
            last = min((self.tile_cols * (q + 1) - 1 + 2 * P_SIZE) // self.step, self.chunks - 1)
            self.pairs += [(q, c) for c in range(first, last + 1)]
        self.parts = 4 if devices % 4 == 0 else 1
        self.ext = pl.cdiv(LANES + self.step * self.chunks + WIN, LANES) * LANES


def send_kernel(plan, design, out, held, arrived):
    lane = lax.broadcasted_iota(jnp.int32, (plan.rows_dev, LANES), 1)
    zero = jnp.zeros((plan.rows_dev, LANES), out.dtype)
    strip, part = plan.strip, plan.width // plan.parts
    copies = [
        pltpu.make_async_copy(design.at[:, pl.ds(i * part, part)], held.at[:, pl.ds(i * part, part)], arrived.at[i])
        for i in range(plan.parts)
    ]
    for copy in copies:
        copy.start()
    for i in range(plan.parts):
        copies[i].wait()
        each = plan.devices // plan.parts
        for s in range(i * each, (i + 1) * each):
            out[s, :, :strip] = held[:, s * strip : (s + 1) * strip]
        for s in range(max(i * each - 1, 0), plan.devices if i == plan.parts - 1 else (i + 1) * each - 1):
            at = s * strip
            before = held[:, at - LANES : at] if s else zero
            after = held[:, at + strip : at + strip + LANES] if s < plan.devices - 1 else zero
            out[s, :, strip:] = jnp.where(lane < LANES // 2, after, before)


def bank_kernel(plan, row_taps, column_taps, interp, shift, phase, rows, columns, up, across, tap_rows, tap_cols, fine, fine_back):
    wide = 3 * LANES
    for held in (tap_rows, tap_cols, fine, fine_back):
        held[...] = jnp.zeros_like(held)
    tap_rows[:, : plan.reach] = row_taps[...].astype(jnp.float32)
    tap_cols[:, : plan.reach] = column_taps[...].astype(jnp.float32)

    def pick(values, side, total=None):
        count = values.shape[side]
        a = lax.broadcasted_iota(jnp.int32, (count, LANES), 0)
        b = lax.broadcasted_iota(jnp.int32, (count, LANES), 1)
        chosen = jnp.where(a == (b if total is None else total - b), 1.0, 0.0).astype(jnp.bfloat16)
        return lax.dot_general(
            values.astype(jnp.bfloat16), chosen, (((side,), (0,)), ((), ())), preferred_element_type=jnp.float32
        )

    tap_cols[:, :LANES] = pick(tap_cols[:, :LANES], 1, plan.reach - 1)
    fine[:, :LANES] = pick(interp[...], 0)
    fine_back[:, :LANES] = pick(interp[...], 0, plan.taps - 1)
    row = lax.broadcasted_iota(jnp.int32, (16, wide), 0)

    def fill(bank, at, taps, moved):
        base = pltpu.roll(jnp.broadcast_to(taps, (16, wide)), ZERO + moved, 1)
        for bit in (1, 2, 4, 8):
            base = jnp.where((row & bit) != 0, pltpu.roll(base, bit, 1), base)
        for m in range(TILES):
            bank[at, 16 * m : 16 * (m + 1), :] = base[:, 16 * (m + 1) : 16 * (m + 1) + LANES].astype(jnp.bfloat16)

    def per_kernel(k, carry):
        fill(rows, k, tap_rows[pl.ds(k, 1), :], 0)
        fill(columns, k, tap_cols[pl.ds(k, 1), :], 0)
        return carry

    lax.fori_loop(0, plan.kernels, per_kernel, 0)
    middle = plan.taps // 2 - 1
    for b in range(plan.blocks):
        fill(up, b, fine[pl.ds(phase[0, 0, b], 1), :], shift[0, 0, b] - middle)
        fill(across, b, fine_back[pl.ds(phase[1, 0, b], 1), :], -shift[1, 0, b])


def band(bank, at, offset, count, cols, used=None):
    assert offset % 16 == 0
    zero = jnp.zeros((16, LANES), jnp.bfloat16)
    tiles = []
    for g in range(count // 16):
        line = []
        for j in range(cols // LANES):
            slot = (LANES * j - 16 * g - offset + ZERO) // 16 - 1
            inside = 0 <= slot < TILES and (used is None or 16 * g < used)
            line.append(bank[at, 16 * slot : 16 * (slot + 1), :] if inside else zero)
        tiles.append(jnp.concatenate(line, axis=1))
    return jnp.concatenate(tiles, axis=0)


def main_kernel(
    plan, design, rows, columns, up, across, weight, care, image, filtered, sums, ext, chunk, intensity, partial, diff
):
    high, pad, tile = plan.height, plan.pad, plan.tile_rows
    strip = plan.strip
    bf16, f32 = jnp.bfloat16, jnp.float32
    place = lax.axis_index("band")
    if pad:
        ext[...] = jnp.zeros_like(ext)
        intensity[...] = jnp.zeros_like(intensity)
    elif plan.ext > strip + 2 * LANES:
        ext[:, strip + 2 * LANES :] = jnp.zeros((high, plan.ext - strip - 2 * LANES), ext.dtype)
    ext[pad : pad + high, :LANES] = design[:, strip:]
    ext[pad : pad + high, LANES : LANES + strip] = design[:, :strip]
    ext[pad : pad + high, LANES + strip : 2 * LANES + strip] = design[:, strip:]
    for c in range(plan.chunks):
        at = LANES - plan.lead + plan.step * c
        chunk[c] = ext[:, at : at + WIN]

    for c in range(plan.chunks):
        column = lax.broadcasted_iota(jnp.int32, (tile, WIN), 1) + (plan.step * c - P_SIZE + place * strip)
        inside = (column >= 0) & (column < plan.width)
        for r in range(plan.row_tiles):
            total = jnp.zeros((tile, WIN), f32)
            for k in range(plan.kernels):
                smooth = jnp.dot(
                    band(rows, k, pad - plan.half, tile, plan.window),
                    chunk[c, tile * r : tile * r + plan.window, :],
                    preferred_element_type=f32,
                ).astype(bf16)
                field = jnp.dot(smooth, band(columns, k, 1 - plan.reach, WIN, WIN), preferred_element_type=f32)
                total = total + weight[k] * field * field
            intensity[c, pad + tile * r : pad + tile * (r + 1), :] = jnp.where(inside, total, 0.0).astype(bf16)
    for c in range(plan.chunks):
        for b in range(plan.blocks):
            at = b * BLK // tile * tile
            partial[c, BLK * b : BLK * (b + 1), :] = jnp.dot(
                band(up, b, pad + b * BLK - at, BLK, plan.window),
                intensity[c, at : at + plan.window, :],
                preferred_element_type=f32,
            ).astype(bf16)

    diff[:8, :] = jnp.zeros((8, strip), f32)
    diff[8 + high :, :] = jnp.zeros((8, strip), f32)
    middle = plan.taps // 2 - 1
    for b in range(plan.blocks):
        cared = care[0, b].astype(f32)
        for q in range(plan.col_tiles):
            warped = jnp.zeros((BLK, plan.tile_cols), f32)
            for tile_at, c in plan.pairs:
                if tile_at == q:
                    offset = plan.step * c - plan.tile_cols * q - P_SIZE + middle - (plan.taps - 1)
                    warped = warped + jnp.dot(
                        partial[c, BLK * b : BLK * (b + 1), :],
                        band(across, b, offset, WIN, plan.tile_cols, plan.step),
                        preferred_element_type=f32,
                    )
            cols = slice(plan.tile_cols * q, plan.tile_cols * (q + 1))
            measured = image[BLK * b : BLK * (b + 1), cols].astype(f32)
            diff[8 + BLK * b : 8 + BLK * (b + 1), cols] = cared * (measured - warped)
    first = jnp.zeros((8, LANES), f32)
    second = jnp.zeros((8, LANES), f32)
    for at in range(0, strip, LANES):
        cols = slice(at, at + LANES)
        value = diff[8 : 8 + high, cols] + 0.5 * (diff[7 : 7 + high, cols] + diff[9 : 9 + high, cols])
        filtered[:, cols] = value
        split = value.reshape(high // 8, 8, LANES)
        first = first + jnp.sum(split, axis=0)
        second = second + jnp.sum(split * split, axis=0)
    both = jnp.concatenate([jnp.sum(first, 0, keepdims=True), jnp.sum(second, 0, keepdims=True)], axis=0)
    for s in range(plan.devices):
        sums[s] = both


def last_kernel(plan, filtered, sums, care, out):
    cells = plan.height * plan.width
    both = jnp.sum(sums[...], axis=0)
    mean = jnp.sum(both[0:1, :]) / cells
    variance = jnp.sum(both[1:2, :]) / cells - mean * mean
    scale = lax.rsqrt(jnp.full((1, LANES), variance + epsilon, jnp.float32))
    for b in range(plan.blocks):
        cared = care[0, b].astype(jnp.float32)
        for at in range(0, plan.strip, LANES):
            value = filtered[BLK * b : BLK * (b + 1), at : at + LANES]
            out[BLK * b : BLK * (b + 1), at : at + LANES] = (cared * ((value - mean) * scale)).astype(out.dtype)


VMEM = pl.BlockSpec(memory_space=pltpu.VMEM)
SMEM = pl.BlockSpec(memory_space=pltpu.SMEM)
FAR = pl.BlockSpec(memory_space=pl.ANY)
GRANT = pltpu.CompilerParams(vmem_limit_bytes=24 << 20)


def near(value):
    return pltpu.with_memory_space_constraint(value, pltpu.VMEM)


def far(value):
    return pltpu.with_memory_space_constraint(value, pltpu.HBM)


def on_device(
    design, row_taps, column_taps, kernel_weight, interp, block_shift, block_phase, care, image
):
    plan = Plan(
        lax.axis_size("band"), design.shape[0], design.shape[1], row_taps.shape[0], row_taps.shape[1], interp.shape[1]
    )
    bf16, f32 = jnp.bfloat16, jnp.float32
    high, strip, kernels = plan.height, plan.strip, plan.kernels
    send = pl.pallas_call(
        functools.partial(send_kernel, plan),
        out_shape=pltpu.VMEM((plan.devices, plan.rows_dev, plan.piece), bf16),
        in_specs=[FAR],
        out_specs=VMEM,
        scratch_shapes=[pltpu.VMEM(design.shape, bf16), pltpu.SemaphoreType.DMA((plan.parts,))],
        compiler_params=GRANT,
    )(far(design))
    got = lax.all_to_all(send, "band", 0, 0, tiled=True).reshape(high, plan.piece)
    bank = lambda count: pltpu.VMEM((count, 16 * TILES, LANES), bf16)
    taps = lambda count: pltpu.VMEM((count, 3 * LANES), f32)
    rows, columns, up, across = pl.pallas_call(
        functools.partial(bank_kernel, plan),
        out_shape=[bank(kernels), bank(kernels), bank(plan.blocks), bank(plan.blocks)],
        in_specs=[VMEM, VMEM, VMEM, SMEM, SMEM],
        out_specs=[VMEM] * 4,
        scratch_shapes=[taps(kernels), taps(kernels), taps(interp.shape[0]), taps(interp.shape[0])],
        compiler_params=GRANT,
        cost_estimate=pl.CostEstimate(flops=10**9, bytes_accessed=8 * 10**6, transcendentals=0),
    )(row_taps, column_taps, interp.T, jnp.swapaxes(block_shift, 1, 2), jnp.swapaxes(block_phase, 1, 2))
    filtered, sums = pl.pallas_call(
        functools.partial(main_kernel, plan),
        out_shape=[pltpu.VMEM((high, strip), f32), pltpu.VMEM((plan.devices, 2, LANES), f32)],
        in_specs=[VMEM] * 5 + [SMEM, SMEM, VMEM],
        out_specs=[VMEM] * 2,
        scratch_shapes=[
            pltpu.VMEM((high + 2 * plan.pad, plan.ext), bf16),
            pltpu.VMEM((plan.chunks, high + 2 * plan.pad, WIN), bf16),
            pltpu.VMEM((plan.chunks, high + 2 * plan.pad, WIN), bf16),
            pltpu.VMEM((plan.chunks, high, WIN), bf16),
            pltpu.VMEM((high + 16, strip), f32),
        ],
        compiler_params=GRANT,
        cost_estimate=pl.CostEstimate(flops=4 * 10**9, bytes_accessed=8 * 10**6, transcendentals=0),
    )(near(got), near(rows), near(columns), near(up), near(across), kernel_weight, care.T, near(image))
    sums = lax.all_to_all(sums, "band", 0, 0, tiled=True)
    return pl.pallas_call(
        functools.partial(last_kernel, plan),
        out_shape=jax.ShapeDtypeStruct((high, strip), bf16),
        in_specs=[VMEM, VMEM, SMEM],
        out_specs=VMEM,
        compiler_params=GRANT,
    )(near(filtered), near(sums), care.T)


def solution(mesh):
    placed = (
        P(("swath", "band"), None),
        P(),
        P(),
        P(),
        P(),
        P(None, "swath", "band"),
        P(None, "swath", "band"),
        P("swath", "band"),
        P("swath", "band"),
    )
    return jax.shard_map(
        on_device, mesh=mesh, in_specs=placed, out_specs=P("swath", "band"), check_vma=False
    )
```

```python
import functools

import jax
import jax.numpy as jnp
from jax import lax
from jax.experimental import pallas as pl
from jax.experimental.pallas import tpu as pltpu
from jax.sharding import PartitionSpec as P

BLK = 128
P_SIZE = 28
LANES = 128
WIN = 256
ZERO = 160
TILES = 12

epsilon = 1e-05


class Plan:
    def __init__(self, devices, rows_dev, width, kernels, reach, taps):
        self.devices, self.rows_dev, self.width = devices, rows_dev, width
        self.kernels, self.reach, self.taps = kernels, reach, taps
        self.half = reach // 2
        self.height = rows_dev * devices
        self.strip = width // devices
        self.piece = self.strip + LANES
        self.blocks = self.height // BLK
        self.tile_rows = min(self.height, 256)
        self.row_tiles = self.height // self.tile_rows
        self.pad = 0 if self.row_tiles == 1 else LANES
        self.window = self.tile_rows + 2 * self.pad
        self.step = WIN - 2 * self.half
        self.tile_cols = min(self.strip, 256)
        self.col_tiles = self.strip // self.tile_cols
        self.chunks = pl.cdiv(self.strip + 2 * P_SIZE, self.step)
        self.lead = P_SIZE + self.half
        self.pairs = []
        for q in range(self.col_tiles):
            first = (self.tile_cols * q + 1) // self.step
            last = min((self.tile_cols * (q + 1) - 1 + 2 * P_SIZE) // self.step, self.chunks - 1)
            self.pairs += [(q, c) for c in range(first, last + 1)]
        self.parts = 4 if devices % 4 == 0 else 1
        self.ext = pl.cdiv(LANES + self.step * self.chunks + WIN, LANES) * LANES


def send_kernel(plan, design, out, held, arrived):
    lane = lax.broadcasted_iota(jnp.int32, (plan.rows_dev, LANES), 1)
    zero = jnp.zeros((plan.rows_dev, LANES), out.dtype)
    strip, part = plan.strip, plan.width // plan.parts
    copies = [
        pltpu.make_async_copy(design.at[:, pl.ds(i * part, part)], held.at[:, pl.ds(i * part, part)], arrived.at[i])
        for i in range(plan.parts)
    ]
    for copy in copies:
        copy.start()
    for i in range(plan.parts):
        copies[i].wait()
        each = plan.devices // plan.parts
        for s in range(i * each, (i + 1) * each):
            out[s, :, :strip] = held[:, s * strip : (s + 1) * strip]
        for s in range(max(i * each - 1, 0), plan.devices if i == plan.parts - 1 else (i + 1) * each - 1):
            at = s * strip
            before = held[:, at - LANES : at] if s else zero
            after = held[:, at + strip : at + strip + LANES] if s < plan.devices - 1 else zero
            out[s, :, strip:] = jnp.where(lane < LANES // 2, after, before)


def bank_kernel(
    plan, row_taps, column_taps, interp, shift, phase, weight, care, rows, columns, up, across, scales, tap_rows, tap_cols, fine, fine_back
):
    wide = 3 * LANES
    for held in (tap_rows, tap_cols, fine, fine_back):
        held[...] = jnp.zeros_like(held)
    tap_rows[:, : plan.reach] = row_taps[...].astype(jnp.float32)
    tap_cols[:, : plan.reach] = column_taps[...].astype(jnp.float32)

    def pick(values, side, total=None):
        count = values.shape[side]
        a = lax.broadcasted_iota(jnp.int32, (count, LANES), 0)
        b = lax.broadcasted_iota(jnp.int32, (count, LANES), 1)
        chosen = jnp.where(a == (b if total is None else total - b), 1.0, 0.0).astype(jnp.bfloat16)
        return lax.dot_general(
            values.astype(jnp.bfloat16), chosen, (((side,), (0,)), ((), ())), preferred_element_type=jnp.float32
        )

    tap_cols[:, :LANES] = pick(tap_cols[:, :LANES], 1, plan.reach - 1)
    fine[:, :LANES] = pick(interp[...], 0)
    fine_back[:, :LANES] = pick(interp[...], 0, plan.taps - 1)
    row = lax.broadcasted_iota(jnp.int32, (16, wide), 0)

    def fill(bank, at, taps, moved):
        base = pltpu.roll(jnp.broadcast_to(taps, (16, wide)), ZERO + moved, 1)
        for bit in (1, 2, 4, 8):
            base = jnp.where((row & bit) != 0, pltpu.roll(base, bit, 1), base)
        for m in range(TILES):
            bank[at, 16 * m : 16 * (m + 1), :] = base[:, 16 * (m + 1) : 16 * (m + 1) + LANES].astype(jnp.bfloat16)

    def per_kernel(k, carry):
        fill(rows, k, tap_rows[pl.ds(k, 1), :], 0)
        fill(columns, k, tap_cols[pl.ds(k, 1), :], 0)
        return carry

    lax.fori_loop(0, plan.kernels, per_kernel, 0)
    middle = plan.taps // 2 - 1
    for b in range(plan.blocks):
        fill(up, b, fine[pl.ds(phase[0, 0, b], 1), :], shift[0, 0, b] - middle)
        fill(across, b, fine_back[pl.ds(phase[1, 0, b], 1), :], -shift[1, 0, b])
    for k in range(plan.kernels):
        scales[k : k + 1, :] = jnp.full((1, WIN), weight[k], jnp.float32)
    for b in range(plan.blocks):
        scales[plan.kernels + b : plan.kernels + b + 1, :] = jnp.full((1, WIN), care[0, b].astype(jnp.float32))


def band(bank, at, offset, count, cols, used=None):
    assert offset % 16 == 0
    zero = jnp.zeros((16, LANES), jnp.bfloat16)
    tiles = []
    for g in range(count // 16):
        line = []
        for j in range(cols // LANES):
            slot = (LANES * j - 16 * g - offset + ZERO) // 16 - 1
            inside = 0 <= slot < TILES and (used is None or 16 * g < used)
            line.append(bank[at, 16 * slot : 16 * (slot + 1), :] if inside else zero)
        tiles.append(jnp.concatenate(line, axis=1))
    return jnp.concatenate(tiles, axis=0)


def main_kernel(
    plan, design, rows, columns, up, across, scales, image, filtered, sums, ext, chunk, intensity, partial, diff
):
    high, pad, tile = plan.height, plan.pad, plan.tile_rows
    strip = plan.strip
    bf16, f32 = jnp.bfloat16, jnp.float32
    place = lax.axis_index("band")
    if pad:
        ext[...] = jnp.zeros_like(ext)
        intensity[...] = jnp.zeros_like(intensity)
    elif plan.ext > strip + 2 * LANES:
        ext[:, strip + 2 * LANES :] = jnp.zeros((high, plan.ext - strip - 2 * LANES), ext.dtype)
    ext[pad : pad + high, :LANES] = design[:, strip:]
    ext[pad : pad + high, LANES : LANES + strip] = design[:, :strip]
    ext[pad : pad + high, LANES + strip : 2 * LANES + strip] = design[:, strip:]
    for c in range(plan.chunks):
        at = LANES - plan.lead + plan.step * c
        chunk[c] = ext[:, at : at + WIN]

    for c in range(plan.chunks):
        column = lax.broadcasted_iota(jnp.int32, (tile, WIN), 1) + (plan.step * c - P_SIZE + place * strip)
        inside = (column >= 0) & (column < plan.width)
        for r in range(plan.row_tiles):
            total = jnp.zeros((tile, WIN), f32)
            for k in range(plan.kernels):
                smooth = jnp.dot(
                    band(rows, k, pad - plan.half, tile, plan.window),
                    chunk[c, tile * r : tile * r + plan.window, :],
                    preferred_element_type=f32,
                ).astype(bf16)
                field = jnp.dot(smooth, band(columns, k, 1 - plan.reach, WIN, WIN), preferred_element_type=f32)
                total = total + scales[k : k + 1, :] * field * field
            intensity[c, pad + tile * r : pad + tile * (r + 1), :] = jnp.where(inside, total, 0.0).astype(bf16)
    for c in range(plan.chunks):
        for b in range(plan.blocks):
            at = b * BLK // tile * tile
            partial[c, BLK * b : BLK * (b + 1), :] = jnp.dot(
                band(up, b, pad + b * BLK - at, BLK, plan.window),
                intensity[c, at : at + plan.window, :],
                preferred_element_type=f32,
            ).astype(bf16)

    diff[:8, :] = jnp.zeros((8, strip), f32)
    diff[8 + high :, :] = jnp.zeros((8, strip), f32)
    middle = plan.taps // 2 - 1
    for b in range(plan.blocks):
        cared = scales[plan.kernels + b : plan.kernels + b + 1, : plan.tile_cols]
        for q in range(plan.col_tiles):
            warped = jnp.zeros((BLK, plan.tile_cols), f32)
            for tile_at, c in plan.pairs:
                if tile_at == q:
                    offset = plan.step * c - plan.tile_cols * q - P_SIZE + middle - (plan.taps - 1)
                    warped = warped + jnp.dot(
                        partial[c, BLK * b : BLK * (b + 1), :],
                        band(across, b, offset, WIN, plan.tile_cols, plan.step),
                        preferred_element_type=f32,
                    )
            cols = slice(plan.tile_cols * q, plan.tile_cols * (q + 1))
            measured = image[BLK * b : BLK * (b + 1), cols].astype(f32)
            diff[8 + BLK * b : 8 + BLK * (b + 1), cols] = cared * (measured - warped)
    first = jnp.zeros((8, LANES), f32)
    second = jnp.zeros((8, LANES), f32)
    for at in range(0, strip, LANES):
        cols = slice(at, at + LANES)
        value = diff[8 : 8 + high, cols] + 0.5 * (diff[7 : 7 + high, cols] + diff[9 : 9 + high, cols])
        filtered[:, cols] = value
        split = value.reshape(high // 8, 8, LANES)
        first = first + jnp.sum(split, axis=0)
        second = second + jnp.sum(split * split, axis=0)
    both = jnp.concatenate([jnp.sum(first, 0, keepdims=True), jnp.sum(second, 0, keepdims=True)], axis=0)
    for s in range(plan.devices):
        sums[s] = both


def last_kernel(plan, filtered, sums, scales, out):
    cells = plan.height * plan.width
    both = jnp.sum(jnp.sum(sums[...], axis=0), axis=1, keepdims=True)
    mean = both[0:1] / cells
    variance = both[1:2] / cells - mean * mean
    scale = lax.rsqrt(variance + epsilon)
    for b in range(plan.blocks):
        factor = scales[plan.kernels + b : plan.kernels + b + 1, 0:1] * scale
        rows = slice(BLK * b, BLK * (b + 1))
        out[rows, :] = ((filtered[rows, :] - mean) * factor).astype(out.dtype)


VMEM = pl.BlockSpec(memory_space=pltpu.VMEM)
SMEM = pl.BlockSpec(memory_space=pltpu.SMEM)
FAR = pl.BlockSpec(memory_space=pl.ANY)
GRANT = pltpu.CompilerParams(vmem_limit_bytes=24 << 20)


def near(value):
    return pltpu.with_memory_space_constraint(value, pltpu.VMEM)


def far(value):
    return pltpu.with_memory_space_constraint(value, pltpu.HBM)


def on_device(
    design, row_taps, column_taps, kernel_weight, interp, block_shift, block_phase, care, image
):
    plan = Plan(
        lax.axis_size("band"), design.shape[0], design.shape[1], row_taps.shape[0], row_taps.shape[1], interp.shape[1]
    )
    bf16, f32 = jnp.bfloat16, jnp.float32
    high, strip, kernels = plan.height, plan.strip, plan.kernels
    send = pl.pallas_call(
        functools.partial(send_kernel, plan),
        out_shape=pltpu.VMEM((plan.devices, plan.rows_dev, plan.piece), bf16),
        in_specs=[FAR],
        out_specs=VMEM,
        scratch_shapes=[pltpu.VMEM(design.shape, bf16), pltpu.SemaphoreType.DMA((plan.parts,))],
        compiler_params=GRANT,
    )(far(design))
    got = lax.all_to_all(send, "band", 0, 0, tiled=True).reshape(high, plan.piece)
    bank = lambda count: pltpu.VMEM((count, 16 * TILES, LANES), bf16)
    taps = lambda count: pltpu.VMEM((count, 3 * LANES), f32)
    rows, columns, up, across, scales = pl.pallas_call(
        functools.partial(bank_kernel, plan),
        out_shape=[bank(kernels), bank(kernels), bank(plan.blocks), bank(plan.blocks), pltpu.VMEM((kernels + plan.blocks, WIN), f32)],
        in_specs=[VMEM, VMEM, VMEM, SMEM, SMEM, SMEM, SMEM],
        out_specs=[VMEM] * 5,
        scratch_shapes=[taps(kernels), taps(kernels), taps(interp.shape[0]), taps(interp.shape[0])],
        compiler_params=GRANT,
        cost_estimate=pl.CostEstimate(flops=10**9, bytes_accessed=8 * 10**6, transcendentals=0),
    )(
        row_taps, column_taps, interp.T, jnp.swapaxes(block_shift, 1, 2), jnp.swapaxes(block_phase, 1, 2),
        kernel_weight, care.T,
    )
    filtered, sums = pl.pallas_call(
        functools.partial(main_kernel, plan),
        out_shape=[pltpu.VMEM((high, strip), f32), pltpu.VMEM((plan.devices, 2, LANES), f32)],
        in_specs=[VMEM] * 7,
        out_specs=[VMEM] * 2,
        scratch_shapes=[
            pltpu.VMEM((high + 2 * plan.pad, plan.ext), bf16),
            pltpu.VMEM((plan.chunks, high + 2 * plan.pad, WIN), bf16),
            pltpu.VMEM((plan.chunks, high + 2 * plan.pad, WIN), bf16),
            pltpu.VMEM((plan.chunks, high, WIN), bf16),
            pltpu.VMEM((high + 16, strip), f32),
        ],
        compiler_params=GRANT,
        cost_estimate=pl.CostEstimate(flops=4 * 10**9, bytes_accessed=8 * 10**6, transcendentals=0),
    )(near(got), near(rows), near(columns), near(up), near(across), near(scales), near(image))
    sums = lax.all_to_all(sums, "band", 0, 0, tiled=True)
    return pl.pallas_call(
        functools.partial(last_kernel, plan),
        out_shape=jax.ShapeDtypeStruct((high, strip), bf16),
        in_specs=[VMEM, VMEM, VMEM],
        out_specs=VMEM,
        compiler_params=GRANT,
    )(near(filtered), near(sums), near(scales))


def solution(mesh):
    placed = (
        P(("swath", "band"), None),
        P(),
        P(),
        P(),
        P(),
        P(None, "swath", "band"),
        P(None, "swath", "band"),
        P("swath", "band"),
        P("swath", "band"),
    )
    return jax.shard_map(
        on_device, mesh=mesh, in_specs=placed, out_specs=P("swath", "band"), check_vma=False
    )
```

```python
import functools

import jax
import jax.numpy as jnp
from jax import lax
from jax.experimental import pallas as pl
from jax.experimental.pallas import tpu as pltpu
from jax.sharding import PartitionSpec as P


BLK = 128
P_SIZE = 28
LANES = 128
WIN = 256
ZERO = 160
CORES = 2
TILES = 12

epsilon = 1e-05


class Plan:
    def __init__(self, devices, rows_dev, width, kernels, reach, taps):
        self.devices, self.rows_dev, self.width = devices, rows_dev, width
        self.kernels, self.reach, self.taps = kernels, reach, taps
        self.half = reach // 2
        self.height = rows_dev * devices
        self.strip = width // devices
        self.piece = self.strip + LANES
        self.blocks = self.height // BLK
        self.tile_rows = min(self.height, 256)
        self.row_tiles = self.height // self.tile_rows
        self.pad = 0 if self.row_tiles == 1 else LANES
        self.window = self.tile_rows + 2 * self.pad
        self.step = WIN - 2 * self.half
        self.tile_cols = min(self.strip, 256)
        self.col_tiles = self.strip // self.tile_cols
        self.chunks = pl.cdiv(self.strip + 2 * P_SIZE, self.step)
        self.lead = P_SIZE + self.half
        self.pairs = []
        for q in range(self.col_tiles):
            first = (self.tile_cols * q + 1) // self.step
            last = min((self.tile_cols * (q + 1) - 1 + 2 * P_SIZE) // self.step, self.chunks - 1)
            self.pairs += [(q, c) for c in range(first, last + 1)]
        self.chips = devices // CORES
        self.union = CORES * self.strip + LANES
        self.ext = pl.cdiv(LANES + self.step * self.chunks + WIN, LANES) * LANES


def partner(chip, hop, chips, back=False):
    if chips & (chips - 1) == 0:
        return chip ^ hop
    return (chip - hop + chips) % chips if back else (chip + hop) % chips


def send_kernel(plan, design, *rest):
    count = (len(rest) - plan.chips - 2) // 2
    small, outs, small_outs = rest[:count], rest[count : count + plan.chips], rest[count + plan.chips : -2]
    held, arrived = rest[-2:]
    lane = lax.broadcasted_iota(jnp.int32, (plan.rows_dev, LANES), 1)
    chip = lax.axis_index("band") // CORES
    copy = pltpu.make_async_copy(design, held.at[:, LANES : LANES + plan.width], arrived.at[0])
    copy.start()
    others = [
        pltpu.make_async_copy(source, out, arrived.at[i + 1]) for i, (source, out) in enumerate(zip(small, small_outs))
    ]
    for other in others:
        other.start()
    held[:, :LANES] = jnp.zeros((plan.rows_dev, LANES), held.dtype)
    held[:, LANES + plan.width :] = jnp.zeros((plan.rows_dev, LANES), held.dtype)
    copy.wait()
    both = CORES * plan.strip
    for hop, out in enumerate(outs):
        at = pl.multiple_of(partner(chip, hop, plan.chips) * both, LANES)
        out[:, :both] = held[:, pl.ds(at + LANES, both)]
        before = held[:, pl.ds(at, LANES)]
        after = held[:, pl.ds(at + LANES + both, LANES)]
        out[:, both:] = jnp.where(lane < LANES // 2, after, before)
    for other in others:
        other.wait()


def strip_of(plan, union, core):
    lane = lax.broadcasted_iota(jnp.int32, (plan.rows_dev, LANES), 1)
    strip = plan.strip
    own = union[:, pl.ds(pl.multiple_of(core * strip, LANES), strip)]
    rim = union[:, CORES * strip :]
    first = jnp.where(lane < LANES // 2, union[:, strip : strip + LANES], rim)
    second = jnp.where(lane < LANES // 2, rim, union[:, strip - LANES : strip])
    return own, jnp.where(core == 0, first, second)


def swap_kernel(plan, *rest):
    unions, out = rest[: plan.chips], rest[plan.chips]
    other = CORES - 1 - lax.rem(lax.axis_index("band"), CORES)
    for hop, union in enumerate(unions):
        own, rims = strip_of(plan, union, other)
        rows = slice(plan.rows_dev * hop, plan.rows_dev * (hop + 1))
        out[rows, : plan.strip] = own
        out[rows, plan.strip :] = rims


def bank_kernel(
    plan, row_taps, column_taps, interp, shift, phase, weight, care, rows, columns, up, across, scales, tap_rows, tap_cols, fine, fine_back
):
    for held in (tap_rows, tap_cols, fine, fine_back):
        held[...] = jnp.zeros_like(held)
    tap_rows[:, : plan.reach] = row_taps[...].astype(jnp.float32)
    tap_cols[:, : plan.reach] = column_taps[...].astype(jnp.float32)

    def pick(values, side, total=None):
        count = values.shape[side]
        a = lax.broadcasted_iota(jnp.int32, (count, LANES), 0)
        b = lax.broadcasted_iota(jnp.int32, (count, LANES), 1)
        chosen = jnp.where(a == (b if total is None else total - b), 1.0, 0.0).astype(jnp.bfloat16)
        return lax.dot_general(
            values.astype(jnp.bfloat16), chosen, (((side,), (0,)), ((), ())), preferred_element_type=jnp.float32
        )

    tap_cols[...] = pick(tap_cols[...], 1, plan.reach - 1)
    fine[...] = pick(interp[...], 0)
    fine_back[...] = pick(interp[...], 0, plan.taps - 1)
    row = lax.broadcasted_iota(jnp.int32, (16, LANES), 0)
    lane = lax.broadcasted_iota(jnp.int32, (16, LANES), 1)

    def fill(bank, at, taps, moved=None):
        base = jnp.broadcast_to(taps, (16, LANES))
        if moved is None:
            base = pltpu.roll(base, ZERO - LANES, 1)
        else:
            ahead = jnp.broadcast_to(moved + (ZERO - LANES), (16, LANES))
            for bit in (1, 2, 4, 8, 16, 32):
                base = jnp.where((ahead & bit) != 0, pltpu.roll(base, bit, 1), base)
        for bit in (1, 2, 4, 8):
            base = jnp.where((row & bit) != 0, pltpu.roll(base, bit, 1), base)
        for m in range(TILES):
            start = LANES - 16 * (m + 1)
            tile = pltpu.roll(base, start % LANES, 1)
            tile = jnp.where(lane >= start if start >= 0 else lane < LANES + start, tile, 0.0)
            bank[at, 16 * m : 16 * (m + 1), :] = tile.astype(jnp.bfloat16)

    def per_kernel(k, carry):
        fill(rows, k, tap_rows[pl.ds(k, 1), :])
        fill(columns, k, tap_cols[pl.ds(k, 1), :])
        return carry

    lax.fori_loop(0, plan.kernels, per_kernel, 0)

    def column(line):
        count = line.shape[1]
        a = lax.broadcasted_iota(jnp.int32, (count, count), 0)
        b = lax.broadcasted_iota(jnp.int32, (count, count), 1)
        return jnp.sum(jnp.where(a == b, jnp.broadcast_to(line, (count, count)), 0.0), axis=1, keepdims=True)

    middle = plan.taps // 2 - 1
    phases = lax.broadcasted_iota(jnp.int32, (plan.blocks, interp.shape[1]), 1).astype(jnp.float32)
    for axis, (held, bank) in enumerate(((fine, up), (fine_back, across))):
        chosen = jnp.where(phases == column(phase[axis].astype(jnp.float32)), 1.0, 0.0).astype(jnp.bfloat16)
        taps = jnp.dot(chosen, held[...].astype(jnp.bfloat16), preferred_element_type=jnp.float32)
        moved = column(shift[axis].astype(jnp.float32)).astype(jnp.int32)
        for b in range(plan.blocks):
            by = moved[b : b + 1]
            fill(bank, b, taps[b : b + 1], by - middle if axis == 0 else -by)
    scales[: plan.kernels, :] = jnp.broadcast_to(column(weight[...]), (plan.kernels, WIN))
    scales[plan.kernels :, :] = jnp.broadcast_to(column(care[...].astype(jnp.float32)), (plan.blocks, WIN))


def band(bank, at, offset, count, cols, used=None):
    assert offset % 16 == 0
    zero = jnp.zeros((16, LANES), jnp.bfloat16)
    tiles = []
    for g in range(count // 16):
        line = []
        for j in range(cols // LANES):
            slot = (LANES * j - 16 * g - offset + ZERO) // 16 - 1
            inside = 0 <= slot < TILES and (used is None or 16 * g < used)
            line.append(bank[at, 16 * slot : 16 * (slot + 1), :] if inside else zero)
        tiles.append(jnp.concatenate(line, axis=1))
    return jnp.concatenate(tiles, axis=0)


def main_kernel(
    plan, *rest
):
    unions, rest = rest[: plan.chips], rest[plan.chips :]
    swapped, rows, columns, up, across, scales, image, filtered, sums, ext, chunk, intensity, partial, diff = rest
    high, pad, tile = plan.height, plan.pad, plan.tile_rows
    strip = plan.strip
    bf16, f32 = jnp.bfloat16, jnp.float32
    place = lax.axis_index("band")
    if pad:
        ext[...] = jnp.zeros_like(ext)
        intensity[...] = jnp.zeros_like(intensity)
    elif plan.ext > strip + 2 * LANES:
        ext[:, strip + 2 * LANES :] = jnp.zeros((high, plan.ext - strip - 2 * LANES), ext.dtype)
    chip, core = place // CORES, lax.rem(place, CORES)
    each = plan.rows_dev
    for hop in range(plan.chips):
        source = partner(chip, hop, plan.chips, True) * CORES
        own, rims = strip_of(plan, unions[hop], core)
        there = swapped[each * hop : each * (hop + 1), :]
        for values, edge, of in ((own, rims, core), (there[:, :strip], there[:, strip:], CORES - 1 - core)):
            at = pl.ds(pl.multiple_of(pad + (source + of) * each, 16), each)
            ext[at, :LANES] = edge
            ext[at, LANES : LANES + strip] = values
            ext[at, LANES + strip : 2 * LANES + strip] = edge
    for c in range(plan.chunks):
        at = LANES - plan.lead + plan.step * c
        chunk[c] = ext[:, at : at + WIN]

    for c in range(plan.chunks):
        column = lax.broadcasted_iota(jnp.int32, (tile, WIN), 1) + (plan.step * c - P_SIZE + place * strip)
        inside = (column >= 0) & (column < plan.width)
        for r in range(plan.row_tiles):
            total = jnp.zeros((tile, WIN), f32)
            for k in range(plan.kernels):
                smooth = jnp.dot(
                    band(rows, k, pad - plan.half, tile, plan.window),
                    chunk[c, tile * r : tile * r + plan.window, :],
                    preferred_element_type=f32,
                ).astype(bf16)
                field = jnp.dot(smooth, band(columns, k, 1 - plan.reach, WIN, WIN), preferred_element_type=f32)
                total = total + scales[k : k + 1, :] * field * field
            intensity[c, pad + tile * r : pad + tile * (r + 1), :] = jnp.where(inside, total, 0.0).astype(bf16)
    for c in range(plan.chunks):
        for b in range(plan.blocks):
            at = b * BLK // tile * tile
            partial[c, BLK * b : BLK * (b + 1), :] = jnp.dot(
                band(up, b, pad + b * BLK - at, BLK, plan.window),
                intensity[c, at : at + plan.window, :],
                preferred_element_type=f32,
            ).astype(bf16)

    diff[:8, :] = jnp.zeros((8, strip), f32)
    diff[8 + high :, :] = jnp.zeros((8, strip), f32)
    middle = plan.taps // 2 - 1
    for b in range(plan.blocks):
        cared = scales[plan.kernels + b : plan.kernels + b + 1, : plan.tile_cols]
        for q in range(plan.col_tiles):
            warped = jnp.zeros((BLK, plan.tile_cols), f32)
            for tile_at, c in plan.pairs:
                if tile_at == q:
                    offset = plan.step * c - plan.tile_cols * q - P_SIZE + middle - (plan.taps - 1)
                    warped = warped + jnp.dot(
                        partial[c, BLK * b : BLK * (b + 1), :],
                        band(across, b, offset, WIN, plan.tile_cols, plan.step),
                        preferred_element_type=f32,
                    )
            cols = slice(plan.tile_cols * q, plan.tile_cols * (q + 1))
            measured = image[BLK * b : BLK * (b + 1), cols].astype(f32)
            diff[8 + BLK * b : 8 + BLK * (b + 1), cols] = cared * (measured - warped)
    first = jnp.zeros((8, LANES), f32)
    second = jnp.zeros((8, LANES), f32)
    for at in range(0, strip, LANES):
        cols = slice(at, at + LANES)
        value = diff[8 : 8 + high, cols] + 0.5 * (diff[7 : 7 + high, cols] + diff[9 : 9 + high, cols])
        filtered[:, cols] = value
        split = value.reshape(high // 8, 8, LANES)
        first = first + jnp.sum(split, axis=0)
        second = second + jnp.sum(split * split, axis=0)
    both = jnp.concatenate([jnp.sum(first, 0, keepdims=True), jnp.sum(second, 0, keepdims=True)], axis=0)
    for s in range(plan.devices):
        sums[s] = both


def last_kernel(plan, filtered, sums, scales, out):
    cells = plan.height * plan.width
    both = jnp.sum(jnp.sum(sums[...], axis=0), axis=1, keepdims=True)
    mean = both[0:1] / cells
    variance = both[1:2] / cells - mean * mean
    scale = lax.rsqrt(variance + epsilon)
    for b in range(plan.blocks):
        factor = scales[plan.kernels + b : plan.kernels + b + 1, 0:1] * scale
        rows = slice(BLK * b, BLK * (b + 1))
        out[rows, :] = ((filtered[rows, :] - mean) * factor).astype(out.dtype)


VMEM = pl.BlockSpec(memory_space=pltpu.VMEM)
SMEM = pl.BlockSpec(memory_space=pltpu.SMEM)
FAR = pl.BlockSpec(memory_space=pl.ANY)
GRANT = pltpu.CompilerParams(vmem_limit_bytes=24 << 20)


def near(value):
    return pltpu.with_memory_space_constraint(value, pltpu.VMEM)


def far(value):
    return pltpu.with_memory_space_constraint(value, pltpu.HBM)


def hops(chips):
    return sorted(range(1, chips), key=lambda hop: (-hop.bit_length(), hop))


def on_device(
    design, row_taps, column_taps, kernel_weight, interp, block_shift, block_phase, care, image
):
    plan = Plan(
        lax.axis_size("band"), design.shape[0], design.shape[1], row_taps.shape[0], row_taps.shape[1], interp.shape[1]
    )
    bf16, f32 = jnp.bfloat16, jnp.float32
    high, strip, kernels = plan.height, plan.strip, plan.kernels
    chips, both = plan.chips, plan.union
    small = (
        row_taps, column_taps, interp.T, jnp.swapaxes(block_shift, 1, 2), jnp.swapaxes(block_phase, 1, 2),
        kernel_weight[None], care.T,
    )
    sent = pl.pallas_call(
        functools.partial(send_kernel, plan),
        out_shape=[pltpu.VMEM((plan.rows_dev, both), bf16)] * chips
        + [pltpu.VMEM(value.shape, value.dtype) for value in small],
        in_specs=[FAR] * (1 + len(small)),
        out_specs=[VMEM] * (chips + len(small)),
        scratch_shapes=[
            pltpu.VMEM((plan.rows_dev, plan.width + 2 * LANES), bf16),
            pltpu.SemaphoreType.DMA((1 + len(small),)),
        ],
        compiler_params=GRANT,
    )(far(design), *[far(value) for value in small])
    unions, small = list(sent[:chips]), sent[chips:]
    for hop in hops(chips):
        pairs = [
            (CORES * chip + core, CORES * partner(chip, hop, chips) + core)
            for chip in range(chips)
            for core in range(CORES)
        ]
        unions[hop] = lax.ppermute(unions[hop], "band", pairs)
    unions = [near(union) for union in unions]
    swapped = pl.pallas_call(
        functools.partial(swap_kernel, plan),
        out_shape=pltpu.VMEM((chips * plan.rows_dev, plan.piece), bf16),
        in_specs=[VMEM] * chips,
        out_specs=VMEM,
        compiler_params=GRANT,
    )(*unions)
    swapped = lax.ppermute(swapped, "band", [(i, i ^ 1) for i in range(plan.devices)])
    bank = lambda count: pltpu.VMEM((count, 16 * TILES, LANES), bf16)
    taps = lambda count: pltpu.VMEM((count, LANES), f32)
    rows, columns, up, across, scales = pl.pallas_call(
        functools.partial(bank_kernel, plan),
        out_shape=[
            bank(kernels), bank(kernels), bank(plan.blocks), bank(plan.blocks),
            pltpu.VMEM((kernels + plan.blocks, WIN), f32),
        ],
        in_specs=[VMEM] * 7,
        out_specs=[VMEM] * 5,
        scratch_shapes=[taps(kernels), taps(kernels), taps(interp.shape[0]), taps(interp.shape[0])],
        compiler_params=GRANT,
        cost_estimate=pl.CostEstimate(flops=10**9, bytes_accessed=8 * 10**6, transcendentals=0),
    )(*[near(value) for value in small])
    filtered, sums = pl.pallas_call(
        functools.partial(main_kernel, plan),
        out_shape=[pltpu.VMEM((high, strip), f32), pltpu.VMEM((plan.devices, 2, LANES), f32)],
        in_specs=[VMEM] * (chips + 7),
        out_specs=[VMEM] * 2,
        scratch_shapes=[
            pltpu.VMEM((high + 2 * plan.pad, plan.ext), bf16),
            pltpu.VMEM((plan.chunks, high + 2 * plan.pad, WIN), bf16),
            pltpu.VMEM((plan.chunks, high + 2 * plan.pad, WIN), bf16),
            pltpu.VMEM((plan.chunks, high, WIN), bf16),
            pltpu.VMEM((high + 16, strip), f32),
        ],
        compiler_params=GRANT,
        cost_estimate=pl.CostEstimate(flops=4 * 10**9, bytes_accessed=8 * 10**6, transcendentals=0),
    )(*unions, near(swapped), near(rows), near(columns), near(up), near(across), near(scales), near(image))
    sums = lax.all_to_all(sums, "band", 0, 0, tiled=True)
    return pl.pallas_call(
        functools.partial(last_kernel, plan),
        out_shape=jax.ShapeDtypeStruct((high, strip), bf16),
        in_specs=[VMEM, VMEM, VMEM],
        out_specs=VMEM,
        compiler_params=GRANT,
    )(near(filtered), near(sums), near(scales))


def solution(mesh):
    placed = (
        P(("swath", "band"), None),
        P(),
        P(),
        P(),
        P(),
        P(None, "swath", "band"),
        P(None, "swath", "band"),
        P("swath", "band"),
        P("swath", "band"),
    )
    return jax.shard_map(
        on_device, mesh=mesh, in_specs=placed, out_specs=P("swath", "band"), check_vma=False
    )
```

```python
import functools

import jax
import jax.numpy as jnp
from jax import lax
from jax.experimental import pallas as pl
from jax.experimental.pallas import tpu as pltpu
from jax.sharding import PartitionSpec as P


BLK = 128
P_SIZE = 28
LANES = 128
WIN = 256
ZERO = 160
CORES = 2
TILES = 12

epsilon = 1e-05


class Plan:
    def __init__(self, devices, rows_dev, width, kernels, reach, taps):
        self.devices, self.rows_dev, self.width = devices, rows_dev, width
        self.kernels, self.reach, self.taps = kernels, reach, taps
        self.half = reach // 2
        self.height = rows_dev * devices
        self.strip = width // devices
        self.piece = self.strip + LANES
        self.blocks = self.height // BLK
        self.tile_rows = min(self.height, 256)
        self.row_tiles = self.height // self.tile_rows
        self.pad = 0 if self.row_tiles == 1 else LANES
        self.window = self.tile_rows + 2 * self.pad
        self.step = WIN - 2 * self.half
        self.tile_cols = min(self.strip, 256)
        self.col_tiles = self.strip // self.tile_cols
        self.chunks = pl.cdiv(self.strip + 2 * P_SIZE, self.step)
        self.lead = P_SIZE + self.half
        self.pairs = []
        for q in range(self.col_tiles):
            first = (self.tile_cols * q + 1) // self.step
            last = min((self.tile_cols * (q + 1) - 1 + 2 * P_SIZE) // self.step, self.chunks - 1)
            self.pairs += [(q, c) for c in range(first, last + 1)]
        self.chips = devices // CORES
        self.union = CORES * self.strip + LANES
        self.ext = pl.cdiv(LANES + self.step * self.chunks + WIN, LANES) * LANES


def partner(chip, hop, chips, back=False):
    if chips & (chips - 1) == 0:
        return chip ^ hop
    return (chip - hop + chips) % chips if back else (chip + hop) % chips


def send_kernel(plan, design, *rest):
    count = (len(rest) - plan.chips - 2) // 2
    small, outs, small_outs = rest[:count], rest[count : count + plan.chips], rest[count + plan.chips : -2]
    held, arrived = rest[-2:]
    lane = lax.broadcasted_iota(jnp.int32, (plan.rows_dev, LANES), 1)
    chip = lax.axis_index("band") // CORES
    copy = pltpu.make_async_copy(design, held.at[:, LANES : LANES + plan.width], arrived.at[0])
    copy.start()
    others = [
        pltpu.make_async_copy(source, out, arrived.at[i + 1]) for i, (source, out) in enumerate(zip(small, small_outs))
    ]
    for other in others:
        other.start()
    held[:, :LANES] = jnp.zeros((plan.rows_dev, LANES), held.dtype)
    held[:, LANES + plan.width :] = jnp.zeros((plan.rows_dev, LANES), held.dtype)
    copy.wait()
    both = CORES * plan.strip
    for hop, out in enumerate(outs):
        at = pl.multiple_of(partner(chip, hop, plan.chips) * both, LANES)
        out[:, :both] = held[:, pl.ds(at + LANES, both)]
        before = held[:, pl.ds(at, LANES)]
        after = held[:, pl.ds(at + LANES + both, LANES)]
        out[:, both:] = jnp.where(lane < LANES // 2, after, before)
    for other in others:
        other.wait()


def strip_of(plan, union, core):
    lane = lax.broadcasted_iota(jnp.int32, (plan.rows_dev, LANES), 1)
    strip = plan.strip
    own = union[:, pl.ds(pl.multiple_of(core * strip, LANES), strip)]
    rim = union[:, CORES * strip :]
    first = jnp.where(lane < LANES // 2, union[:, strip : strip + LANES], rim)
    second = jnp.where(lane < LANES // 2, rim, union[:, strip - LANES : strip])
    return own, jnp.where(core == 0, first, second)


def swap_kernel(plan, *rest):
    unions, out = rest[: plan.chips], rest[plan.chips]
    other = CORES - 1 - lax.rem(lax.axis_index("band"), CORES)
    for hop, union in enumerate(unions):
        own, rims = strip_of(plan, union, other)
        rows = slice(plan.rows_dev * hop, plan.rows_dev * (hop + 1))
        out[rows, : plan.strip] = own
        out[rows, plan.strip :] = rims


def bank_kernel(
    plan, row_taps, column_taps, interp, shift, phase, weight, care, rows, columns, up, across, scales, tap_rows, tap_cols, fine, fine_back
):
    for held in (tap_rows, tap_cols, fine, fine_back):
        held[...] = jnp.zeros_like(held)
    tap_rows[:, : plan.reach] = row_taps[...].astype(jnp.float32)
    tap_cols[:, : plan.reach] = column_taps[...].astype(jnp.float32)

    def pick(values, side, total=None):
        count = values.shape[side]
        a = lax.broadcasted_iota(jnp.int32, (count, LANES), 0)
        b = lax.broadcasted_iota(jnp.int32, (count, LANES), 1)
        chosen = jnp.where(a == (b if total is None else total - b), 1.0, 0.0).astype(jnp.bfloat16)
        return lax.dot_general(
            values.astype(jnp.bfloat16), chosen, (((side,), (0,)), ((), ())), preferred_element_type=jnp.float32
        )

    tap_cols[...] = pick(tap_cols[...], 1, plan.reach - 1)
    fine[...] = pick(interp[...], 0)
    fine_back[...] = pick(interp[...], 0, plan.taps - 1)
    row = lax.broadcasted_iota(jnp.int32, (16, LANES), 0)
    lane = lax.broadcasted_iota(jnp.int32, (16, LANES), 1)

    def fill(bank, at, taps, moved=None):
        base = jnp.broadcast_to(taps, (16, LANES))
        if moved is None:
            base = pltpu.roll(base, ZERO - LANES, 1)
        else:
            ahead = jnp.broadcast_to(moved + (ZERO - LANES), (16, LANES))
            for bit in (1, 2, 4, 8, 16, 32):
                base = jnp.where((ahead & bit) != 0, pltpu.roll(base, bit, 1), base)
        for bit in (1, 2, 4, 8):
            base = jnp.where((row & bit) != 0, pltpu.roll(base, bit, 1), base)
        for m in range(TILES):
            start = LANES - 16 * (m + 1)
            tile = pltpu.roll(base, start % LANES, 1)
            tile = jnp.where(lane >= start if start >= 0 else lane < LANES + start, tile, 0.0)
            bank[at, 16 * m : 16 * (m + 1), :] = tile.astype(jnp.bfloat16)

    for k in range(plan.kernels):
        fill(rows, k, tap_rows[k : k + 1, :])
        fill(columns, k, tap_cols[k : k + 1, :])

    def column(line):
        count = line.shape[1]
        a = lax.broadcasted_iota(jnp.int32, (count, count), 0)
        b = lax.broadcasted_iota(jnp.int32, (count, count), 1)
        return jnp.sum(jnp.where(a == b, jnp.broadcast_to(line, (count, count)), 0.0), axis=1, keepdims=True)

    middle = plan.taps // 2 - 1
    phases = lax.broadcasted_iota(jnp.int32, (plan.blocks, interp.shape[1]), 1).astype(jnp.float32)
    for axis, (held, bank) in enumerate(((fine, up), (fine_back, across))):
        chosen = jnp.where(phases == column(phase[axis].astype(jnp.float32)), 1.0, 0.0).astype(jnp.bfloat16)
        taps = jnp.dot(chosen, held[...].astype(jnp.bfloat16), preferred_element_type=jnp.float32)
        moved = column(shift[axis].astype(jnp.float32)).astype(jnp.int32)
        for b in range(plan.blocks):
            by = moved[b : b + 1]
            fill(bank, b, taps[b : b + 1], by - middle if axis == 0 else -by)
    scales[: plan.kernels, :] = jnp.broadcast_to(column(weight[...]), (plan.kernels, WIN))
    scales[plan.kernels :, :] = jnp.broadcast_to(column(care[...].astype(jnp.float32)), (plan.blocks, WIN))


def band(bank, at, offset, count, cols, used=None):
    assert offset % 16 == 0
    zero = jnp.zeros((16, LANES), jnp.bfloat16)
    tiles = []
    for g in range(count // 16):
        line = []
        for j in range(cols // LANES):
            slot = (LANES * j - 16 * g - offset + ZERO) // 16 - 1
            inside = 0 <= slot < TILES and (used is None or 16 * g < used)
            line.append(bank[at, 16 * slot : 16 * (slot + 1), :] if inside else zero)
        tiles.append(jnp.concatenate(line, axis=1))
    return jnp.concatenate(tiles, axis=0)


def main_kernel(
    plan, *rest
):
    unions, rest = rest[: plan.chips], rest[plan.chips :]
    swapped, rows, columns, up, across, scales, image, filtered, sums, ext, chunk, intensity, partial, diff = rest
    high, pad, tile = plan.height, plan.pad, plan.tile_rows
    strip = plan.strip
    bf16, f32 = jnp.bfloat16, jnp.float32
    place = lax.axis_index("band")
    if pad:
        ext[...] = jnp.zeros_like(ext)
        intensity[...] = jnp.zeros_like(intensity)
    elif plan.ext > strip + 2 * LANES:
        ext[:, strip + 2 * LANES :] = jnp.zeros((high, plan.ext - strip - 2 * LANES), ext.dtype)
    chip, core = place // CORES, lax.rem(place, CORES)
    each = plan.rows_dev
    for hop in range(plan.chips):
        source = partner(chip, hop, plan.chips, True) * CORES
        own, rims = strip_of(plan, unions[hop], core)
        there = swapped[each * hop : each * (hop + 1), :]
        for values, edge, of in ((own, rims, core), (there[:, :strip], there[:, strip:], CORES - 1 - core)):
            at = pl.ds(pl.multiple_of(pad + (source + of) * each, 16), each)
            ext[at, :LANES] = edge
            ext[at, LANES : LANES + strip] = values
            ext[at, LANES + strip : 2 * LANES + strip] = edge
    for c in range(plan.chunks):
        at = LANES - plan.lead + plan.step * c
        chunk[c] = ext[:, at : at + WIN]

    for c in range(plan.chunks):
        column = lax.broadcasted_iota(jnp.int32, (tile, WIN), 1) + (plan.step * c - P_SIZE + place * strip)
        inside = (column >= 0) & (column < plan.width)
        for r in range(plan.row_tiles):
            total = jnp.zeros((tile, WIN), f32)
            for k in range(plan.kernels):
                smooth = jnp.dot(
                    band(rows, k, pad - plan.half, tile, plan.window),
                    chunk[c, tile * r : tile * r + plan.window, :],
                    preferred_element_type=f32,
                ).astype(bf16)
                field = jnp.dot(smooth, band(columns, k, 1 - plan.reach, WIN, WIN), preferred_element_type=f32)
                total = total + scales[k : k + 1, :] * field * field
            intensity[c, pad + tile * r : pad + tile * (r + 1), :] = jnp.where(inside, total, 0.0).astype(bf16)
    for c in range(plan.chunks):
        for b in range(plan.blocks):
            at = b * BLK // tile * tile
            partial[c, BLK * b : BLK * (b + 1), :] = jnp.dot(
                band(up, b, pad + b * BLK - at, BLK, plan.window),
                intensity[c, at : at + plan.window, :],
                preferred_element_type=f32,
            ).astype(bf16)

    diff[:8, :] = jnp.zeros((8, strip), f32)
    diff[8 + high :, :] = jnp.zeros((8, strip), f32)
    middle = plan.taps // 2 - 1
    for b in range(plan.blocks):
        cared = scales[plan.kernels + b : plan.kernels + b + 1, : plan.tile_cols]
        for q in range(plan.col_tiles):
            warped = jnp.zeros((BLK, plan.tile_cols), f32)
            for tile_at, c in plan.pairs:
                if tile_at == q:
                    offset = plan.step * c - plan.tile_cols * q - P_SIZE + middle - (plan.taps - 1)
                    warped = warped + jnp.dot(
                        partial[c, BLK * b : BLK * (b + 1), :],
                        band(across, b, offset, WIN, plan.tile_cols, plan.step),
                        preferred_element_type=f32,
                    )
            cols = slice(plan.tile_cols * q, plan.tile_cols * (q + 1))
            measured = image[BLK * b : BLK * (b + 1), cols].astype(f32)
            diff[8 + BLK * b : 8 + BLK * (b + 1), cols] = cared * (measured - warped)
    first = jnp.zeros((8, LANES), f32)
    second = jnp.zeros((8, LANES), f32)
    for at in range(0, strip, LANES):
        cols = slice(at, at + LANES)
        value = diff[8 : 8 + high, cols] + 0.5 * (diff[7 : 7 + high, cols] + diff[9 : 9 + high, cols])
        filtered[:, cols] = value
        split = value.reshape(high // 8, 8, LANES)
        first = first + jnp.sum(split, axis=0)
        second = second + jnp.sum(split * split, axis=0)
    both = jnp.concatenate([jnp.sum(first, 0, keepdims=True), jnp.sum(second, 0, keepdims=True)], axis=0)
    for s in range(plan.devices):
        sums[s] = both


def last_kernel(plan, filtered, sums, scales, out):
    cells = plan.height * plan.width
    both = jnp.sum(jnp.sum(sums[...], axis=0), axis=1, keepdims=True)
    mean = both[0:1] / cells
    variance = both[1:2] / cells - mean * mean
    scale = lax.rsqrt(variance + epsilon)
    for b in range(plan.blocks):
        factor = scales[plan.kernels + b : plan.kernels + b + 1, 0:1] * scale
        rows = slice(BLK * b, BLK * (b + 1))
        out[rows, :] = ((filtered[rows, :] - mean) * factor).astype(out.dtype)


VMEM = pl.BlockSpec(memory_space=pltpu.VMEM)
SMEM = pl.BlockSpec(memory_space=pltpu.SMEM)
FAR = pl.BlockSpec(memory_space=pl.ANY)
GRANT = pltpu.CompilerParams(vmem_limit_bytes=24 << 20)


def near(value):
    return pltpu.with_memory_space_constraint(value, pltpu.VMEM)


def far(value):
    return pltpu.with_memory_space_constraint(value, pltpu.HBM)


def hops(chips):
    half = chips // 2
    return sorted(range(1, chips), key=lambda hop: (hop < half, (hop & 1) ^ (hop < half), -hop))


def on_device(
    design, row_taps, column_taps, kernel_weight, interp, block_shift, block_phase, care, image
):
    plan = Plan(
        lax.axis_size("band"), design.shape[0], design.shape[1], row_taps.shape[0], row_taps.shape[1], interp.shape[1]
    )
    bf16, f32 = jnp.bfloat16, jnp.float32
    high, strip, kernels = plan.height, plan.strip, plan.kernels
    chips, both = plan.chips, plan.union
    small = (
        row_taps, column_taps, interp.T, jnp.swapaxes(block_shift, 1, 2), jnp.swapaxes(block_phase, 1, 2),
        kernel_weight[None], care.T,
    )
    sent = pl.pallas_call(
        functools.partial(send_kernel, plan),
        out_shape=[pltpu.VMEM((plan.rows_dev, both), bf16)] * chips
        + [pltpu.VMEM(value.shape, value.dtype) for value in small],
        in_specs=[FAR] * (1 + len(small)),
        out_specs=[VMEM] * (chips + len(small)),
        scratch_shapes=[
            pltpu.VMEM((plan.rows_dev, plan.width + 2 * LANES), bf16),
            pltpu.SemaphoreType.DMA((1 + len(small),)),
        ],
        compiler_params=GRANT,
    )(far(design), *[far(value) for value in small])
    unions, small = list(sent[:chips]), sent[chips:]
    for hop in hops(chips):
        pairs = [
            (CORES * chip + core, CORES * partner(chip, hop, chips) + core)
            for chip in range(chips)
            for core in range(CORES)
        ]
        unions[hop] = lax.ppermute(unions[hop], "band", pairs)
    unions = [near(union) for union in unions]
    swapped = pl.pallas_call(
        functools.partial(swap_kernel, plan),
        out_shape=pltpu.VMEM((chips * plan.rows_dev, plan.piece), bf16),
        in_specs=[VMEM] * chips,
        out_specs=VMEM,
        compiler_params=GRANT,
    )(*unions)
    swapped = lax.ppermute(swapped, "band", [(i, i ^ 1) for i in range(plan.devices)])
    bank = lambda count: pltpu.VMEM((count, 16 * TILES, LANES), bf16)
    taps = lambda count: pltpu.VMEM((count, LANES), f32)
    rows, columns, up, across, scales = pl.pallas_call(
        functools.partial(bank_kernel, plan),
        out_shape=[
            bank(kernels), bank(kernels), bank(plan.blocks), bank(plan.blocks),
            pltpu.VMEM((kernels + plan.blocks, WIN), f32),
        ],
        in_specs=[VMEM] * 7,
        out_specs=[VMEM] * 5,
        scratch_shapes=[taps(kernels), taps(kernels), taps(interp.shape[0]), taps(interp.shape[0])],
        compiler_params=GRANT,
        cost_estimate=pl.CostEstimate(flops=10**9, bytes_accessed=8 * 10**6, transcendentals=0),
    )(*[near(value) for value in small])
    filtered, sums = pl.pallas_call(
        functools.partial(main_kernel, plan),
        out_shape=[pltpu.VMEM((high, strip), f32), pltpu.VMEM((plan.devices, 2, LANES), f32)],
        in_specs=[VMEM] * (chips + 7),
        out_specs=[VMEM] * 2,
        scratch_shapes=[
            pltpu.VMEM((high + 2 * plan.pad, plan.ext), bf16),
            pltpu.VMEM((plan.chunks, high + 2 * plan.pad, WIN), bf16),
            pltpu.VMEM((plan.chunks, high + 2 * plan.pad, WIN), bf16),
            pltpu.VMEM((plan.chunks, high, WIN), bf16),
            pltpu.VMEM((high + 16, strip), f32),
        ],
        compiler_params=GRANT,
        cost_estimate=pl.CostEstimate(flops=4 * 10**9, bytes_accessed=8 * 10**6, transcendentals=0),
    )(*unions, near(swapped), near(rows), near(columns), near(up), near(across), near(scales), near(image))
    sums = lax.all_to_all(sums, "band", 0, 0, tiled=True)
    return pl.pallas_call(
        functools.partial(last_kernel, plan),
        out_shape=jax.ShapeDtypeStruct((high, strip), bf16),
        in_specs=[VMEM, VMEM, VMEM],
        out_specs=VMEM,
        compiler_params=GRANT,
    )(near(filtered), near(sums), near(scales))


def solution(mesh):
    placed = (
        P(("swath", "band"), None),
        P(),
        P(),
        P(),
        P(),
        P(None, "swath", "band"),
        P(None, "swath", "band"),
        P("swath", "band"),
        P("swath", "band"),
    )
    return jax.shard_map(
        on_device, mesh=mesh, in_specs=placed, out_specs=P("swath", "band"), check_vma=False
    )
```
